1024 devices in a mesh: section: 32 (over x_hi, z), tp: 8 (over y), dp: 4 (over x_lo, core).
Axes of the slice: x: 4 (x_hi: 2, x_lo: 2; x = x_hi * 2 + x_lo), y: 8, z: 16, core: 2. Of those that a mesh axis runs over, the one named last changes fastest.
Arguments:
- incoming: bfloat16 [32, 32, 128, 2304], P('section', ('dp', 'tp')), parts along dimension 1, may hold values from -6 to 6
- fresh_rows: bfloat16 [6, 32, 128, 2304], P(None, ('dp', 'tp')), parts along dimension 1, may hold values from -6 to 6
- entry_order: int32 [24], P('dp'), parts along dimension 0, may hold values from 0 to 5, each once
- flight_lengths: int32 [32, 32], P('section', 'dp'), parts along dimension 1, may hold values from 16 to 128
- pre_gain: float32 [32, 2304], P('section'), may hold values from 0.1 to 1.9
- post_gain: float32 [32, 2304], P('section'), may hold values from 0.1 to 1.9
- w_query: bfloat16 [32, 2304, 2048], P('section', None, 'tp'), may hold values from -0.125 to 0.125
- key_weight: bfloat16 [32, 2304, 1024], P('section', None, 'tp'), may hold values from -0.125 to 0.125
- value_weight: bfloat16 [32, 2304, 1024], P('section', None, 'tp'), may hold values from -0.125 to 0.125
- w_out: bfloat16 [32, 2048, 2304], P('section', 'tp'), may hold values from -0.125 to 0.125
Outputs:
- produced: bfloat16 [32, 32, 128, 2304], P('section', ('dp', 'tp')), parts along dimension 1
- advanced: bfloat16 [32, 32, 128, 2304], P('section', ('dp', 'tp')), parts along dimension 1
The draws below stay inside these ranges and needn't reach their ends.
There are 4 independent parts, one for each index of `dp`. The reference program is written for one: setup_inputs(seed, part) draws one part's arguments, and reference() takes and returns one part's arrays. A program takes and returns all parts, laid end to end along the dimension named above; an argument that names none is the same for every part. Nothing has to cross between parts.
Inputs may be any that keep to these rules, and one draw needn't show every extreme that they name: `entry_order`: each waiting microbatch appears once.
All inputs are finite; a program needn't handle non-finite values.
Results may differ from the reference program's by a relative error of at most 0.012.
Values may be sent and summed in bfloat16 or wider, within the bound.
A program may use at most 64 MiB of HBM per device.

```python
import jax
import jax.numpy as jnp
from jax import lax

MODEL_WIDTH = 2304
QUERY_HEADS = 16
KEY_VALUE_HEADS = 8
HEAD_WIDTH = 128
SEQUENCE_TOKENS = 128
POOL = 6
MICRO_SEQUENCES = 8
N_SECTION = 32
N_TP = 8


def set_ends(result, rng, least, top_value):
    place = [jax.random.randint(jax.random.fold_in(rng, axis), (), 0, length) for axis, length in enumerate(result.shape)]
    main_axis = result.shape.index(max(result.shape))
    beside = place[:main_axis] + [(place[main_axis] + 1) % result.shape[main_axis]] + place[main_axis + 1:]
    return result.at[tuple(place)].set(least).at[tuple(beside)].set(top_value)


def shard_levels(stream_key, extent, cuts, smallest, largest):
    level = 1.0
    for axis_at, blocks in cuts:
        heights = jax.random.uniform(jax.random.fold_in(jax.random.fold_in(stream_key, 6), axis_at), (blocks,), jnp.float32, smallest / len(cuts), largest / len(cuts))
        level = level * jnp.repeat(jnp.exp(heights), extent[axis_at] // blocks).reshape((-1,) + (1,) * (len(extent) - 1 - axis_at))
    return level


def normal_values(rng, shape, scale, bound, pieces=(), kind=jnp.bfloat16):
    factor_of = shard_levels(rng, shape, pieces, -0.22, 0.18) if pieces else 1.0
    values = jax.random.normal(rng, shape, jnp.float32) * scale * factor_of
    return jnp.minimum(jnp.maximum(values, -bound), bound).astype(kind)


def setup_inputs(seed: int = 0, part: int = 0) -> dict:
    splits = jax.random.split(jax.random.key(seed), 11)
    part_keys = jax.random.split(jax.random.fold_in(splits[10], part), 11)
    return {
        "incoming": normal_values(part_keys[0], (N_SECTION, MICRO_SEQUENCES, SEQUENCE_TOKENS, MODEL_WIDTH), 1.0, 6.0, ((0, 32), (1, 8))),
        "fresh_rows": normal_values(part_keys[1], (POOL, MICRO_SEQUENCES, SEQUENCE_TOKENS, MODEL_WIDTH), 1.0, 6.0, ((1, 8),)),
        "entry_order": jax.random.permutation(part_keys[2], POOL).astype(jnp.int32),
        "flight_lengths": set_ends(jax.random.randint(part_keys[3], (N_SECTION, MICRO_SEQUENCES), SEQUENCE_TOKENS // 8, SEQUENCE_TOKENS + 1), jax.random.fold_in(part_keys[3], 1), SEQUENCE_TOKENS // 8, SEQUENCE_TOKENS).astype(jnp.int32),
        "pre_gain": jnp.clip(1.0 + 0.18 * jax.random.normal(splits[4], (N_SECTION, MODEL_WIDTH), jnp.float32), 0.1, 1.9),
        "post_gain": jnp.clip(1.0 + 0.18 * jax.random.normal(splits[5], (N_SECTION, MODEL_WIDTH), jnp.float32), 0.1, 1.9),
        "w_query": normal_values(splits[6], (N_SECTION, MODEL_WIDTH, QUERY_HEADS * HEAD_WIDTH), MODEL_WIDTH ** -0.5, 0.125, ((0, 32), (2, 8))),
        "key_weight": normal_values(splits[7], (N_SECTION, MODEL_WIDTH, KEY_VALUE_HEADS * HEAD_WIDTH), MODEL_WIDTH ** -0.5, 0.125, ((0, 32), (2, 8))),
        "value_weight": normal_values(splits[8], (N_SECTION, MODEL_WIDTH, KEY_VALUE_HEADS * HEAD_WIDTH), MODEL_WIDTH ** -0.5, 0.125, ((0, 32), (2, 8))),
        "w_out": normal_values(splits[9], (N_SECTION, QUERY_HEADS * HEAD_WIDTH, MODEL_WIDTH), (QUERY_HEADS * HEAD_WIDTH) ** -0.5, 0.125, ((0, 32), (1, 8))),
    }


EPSILON = 1e-06
SOFT_CAP = 50.0
QUERY_SCALE = 144.0 ** (-0.5)

def normalize(values, gain):
    return values * lax.rsqrt(lax.optimization_barrier(jnp.mean(values * values, -1, keepdims=True)) + EPSILON) * gain

def apply_rotary(values, token_positions):
    half = values.shape[-1] // 2
    freq = 10000.0 ** (-2.0 * jnp.arange(half).astype(jnp.float32) / values.shape[-1])
    angle = token_positions[:, None].astype(jnp.float32) * freq[None, :]
    cosine = jnp.cos(angle)[:, None, :]
    sine = jnp.sin(angle)[:, None, :]
    first = values[..., :half]
    second = values[..., half:]
    return jnp.concatenate([first * cosine - second * sine, second * cosine + first * sine], -1)

def layer(held, lengths, gain_before, gain_after, w_query, key_weight, value_weight, w_out):
    widened = held.astype(jnp.float32).reshape(MICRO_SEQUENCES * SEQUENCE_TOKENS, MODEL_WIDTH)
    normalized_input = normalize(widened, gain_before).astype(jnp.bfloat16)
    token_positions = jnp.tile(jnp.arange(SEQUENCE_TOKENS).astype(jnp.int32), MICRO_SEQUENCES)
    query_matrix = jnp.dot(normalized_input, w_query, preferred_element_type=jnp.float32).reshape(MICRO_SEQUENCES * SEQUENCE_TOKENS, QUERY_HEADS, HEAD_WIDTH)
    query_matrix = apply_rotary(query_matrix, token_positions).astype(jnp.bfloat16).reshape(MICRO_SEQUENCES, SEQUENCE_TOKENS, KEY_VALUE_HEADS, QUERY_HEADS // KEY_VALUE_HEADS, HEAD_WIDTH)
    projected_keys = apply_rotary(jnp.dot(normalized_input, key_weight, preferred_element_type=jnp.float32).reshape(MICRO_SEQUENCES * SEQUENCE_TOKENS, KEY_VALUE_HEADS, HEAD_WIDTH), token_positions).astype(jnp.bfloat16).reshape(MICRO_SEQUENCES, SEQUENCE_TOKENS, KEY_VALUE_HEADS, HEAD_WIDTH)
    projected_values = jnp.dot(normalized_input, value_weight, preferred_element_type=jnp.float32).astype(jnp.bfloat16).reshape(MICRO_SEQUENCES, SEQUENCE_TOKENS, KEY_VALUE_HEADS, HEAD_WIDTH)
    scores = jnp.einsum('bqkgd,bskd->bkgqs', query_matrix.astype(jnp.float32), projected_keys.astype(jnp.float32)) * QUERY_SCALE
    capped = SOFT_CAP * jnp.tanh(scores / SOFT_CAP)
    position = jnp.arange(SEQUENCE_TOKENS).astype(jnp.int32)
    causal = position[None, :] <= position[:, None]
    allowed = causal[None, :, :] & (position[None, None, :] < lengths[:, None, None])
    raised = jnp.where(allowed[:, None, None, :, :], jnp.exp(capped), jnp.float32(0.0))
    probs = (raised / lax.optimization_barrier(jnp.sum(raised, -1, keepdims=True))).astype(jnp.bfloat16)
    mixed = jnp.einsum('bkgqs,bskd->bqkgd', probs.astype(jnp.float32), projected_values.astype(jnp.float32)).astype(jnp.bfloat16)
    mixed = mixed.reshape(MICRO_SEQUENCES * SEQUENCE_TOKENS, N_TP, QUERY_HEADS * HEAD_WIDTH // N_TP)
    grouped = jnp.einsum('sjc,jcd->jsd', mixed.astype(jnp.float32), w_out.reshape(N_TP, QUERY_HEADS * HEAD_WIDTH // N_TP, MODEL_WIDTH).astype(jnp.float32))
    grouped = lax.optimization_barrier(grouped.astype(jnp.bfloat16))
    branch_sum = lax.optimization_barrier(jnp.sum(grouped.astype(jnp.float32), 0))
    return (widened + normalize(branch_sum, gain_after)).astype(jnp.bfloat16).reshape(MICRO_SEQUENCES, SEQUENCE_TOKENS, MODEL_WIDTH)

def reference(incoming, fresh_rows, entry_order, flight_lengths, pre_gain, post_gain, w_query, key_weight, value_weight, w_out):

    def section_step(section):
        return layer(incoming[section], flight_lengths[section], pre_gain[section], post_gain[section], w_query[section], key_weight[section], value_weight[section], w_out[section])
    produced = lax.map(section_step, jnp.arange(N_SECTION).astype(jnp.int32))
    chosen = entry_order[0]
    advanced = jnp.concatenate([fresh_rows[chosen][None], produced[:-1]], 0)
    return (produced, advanced)
```

```python
import functools

import jax
import jax.numpy as jnp
import numpy as np
from jax import lax
from jax.experimental import pallas as pl
from jax.experimental.pallas import tpu as pltpu
from jax.sharding import PartitionSpec as P

HEAD_WIDTH = 128
EPSILON = 1e-06
SOFT_CAP = 50.0
QUERY_SCALE = 144.0 ** (-0.5)
MESH = pl.DeviceIdType.MESH
CHUNKS = 4

STEPS = [
    ("A", 0, 0), ("D", 0), ("A", 1, 0),
    ("U", 0, 0), ("A", 0, 1), ("U", 1, 0), ("U", 0, 1),
    ("D", 1), ("A", 1, 1), ("U", 1, 1),
    ("A", 0, 2), ("U", 0, 2), ("D", 2), ("X", 0), ("A", 1, 2), ("U", 1, 2),
    ("A", 0, 3), ("A", 2, 0), ("U", 0, 3), ("D", 3), ("X", 1), ("A", 1, 3), ("U", 1, 3), ("A", 3, 0),
    ("A", 0, 4), ("U", 0, 4), ("D", 4), ("A", 1, 4), ("U", 1, 4), ("U", 2, 0), ("U", 3, 0),
    ("A", 2, 1), ("U", 2, 1), ("A", 3, 1), ("X", 2), ("U", 3, 1), ("A", 2, 2), ("X", 3),
    ("U", 2, 2), ("A", 3, 2), ("U", 3, 2), ("W",), ("O", 0), ("A", 2, 3), ("U", 2, 3), ("O", 1), ("A", 3, 3), ("U", 3, 3),
    ("A", 2, 4), ("U", 2, 4), ("A", 3, 4), ("U", 3, 4), ("O", 2), ("O", 3),
]


def kernel(
    n_section, lens, x, gain_before, gain_after, cosine, sine, wq, wk, wv, wo,
    produced, received,
    xg, wqkv, wout, keys, values, normed, outgoing, mixed, branch, made, g1, g2, cs, sn,
    a_send, a_recv, d_send, d_recv, x_send, x_recv, e_send, e_recv, f_send, f_recv, c_send, c_recv,
    z_send, z_recv, l_sem, o_sem,
):
    n_tp = wout.shape[0]
    section = lax.axis_index("section")
    t = lax.axis_index("tp")
    dp = lax.axis_index("dp")
    seq, width = x.shape
    rows = seq // CHUNKS
    group = wo.shape[0]
    quarter = group // 4
    kv = wk.shape[1]
    other_core = dp + 1 - 2 * lax.rem(dp, 2)
    beside = lax.rem(dp + 2, 4)

    def at_tp(distance):
        return lax.rem(t + n_tp + distance, n_tp)

    sources = (x, wq, wk, wv, wo, gain_before, gain_after, cosine, sine)
    targets = (
        xg.at[t], wqkv.at[:, :group], wqkv.at[:, group:group + kv], wqkv.at[:, group + kv:], wout.at[t], g1, g2, cs, sn,
    )
    local = [pltpu.make_async_copy(s, d, l_sem.at[i]) for i, (s, d) in enumerate(zip(sources, targets))]
    for copy in local:
        copy.start()

    barrier = pltpu.get_barrier_semaphore()
    for distance in range(1, n_tp):
        pl.semaphore_signal(barrier, inc=1, device_id={"tp": at_tp(distance)}, device_id_type=MESH)
    pl.semaphore_signal(barrier, inc=1, device_id={"dp": other_core}, device_id_type=MESH)
    pl.semaphore_signal(barrier, inc=1, device_id={"dp": beside}, device_id_type=MESH)

    for distance in (1, n_section - 1):
        pl.semaphore_signal(
            barrier, inc=1, device_id={"section": lax.rem(section + distance, n_section)}, device_id_type=MESH
        )
    pl.semaphore_wait(barrier, n_tp + 3)

    pending = []

    def remote(src, dst, send, recv, device):
        return pltpu.make_async_remote_copy(
            src_ref=src, dst_ref=dst, send_sem=send, recv_sem=recv, device_id=device, device_id_type=MESH
        )

    def start(copy):
        copy.start()
        pending.append(copy)

    def ring_rows(way, c, h):
        if h < 3:
            return pl.ds(c * rows, rows)
        return pl.ds(c * rows + way * (rows // 2), rows // 2)

    def ring(way, c, h, arriving):
        sign = 1 if way == 0 else -1
        block = at_tp(-sign * (h + 1 if arriving else h))
        part = xg.at[block, ring_rows(way, c, h)]
        src = x.at[ring_rows(way, c, h)] if h == 0 and not arriving else part
        return remote(src, part, a_send.at[way, c, h], a_recv.at[way, c, h], {"tp": at_tp(sign)})

    def weight_rows(who, way, h):
        if h < 3:
            return pl.ds(who * quarter, quarter)
        return pl.ds(who * quarter + way * (quarter // 2), quarter // 2)

    def weight_part(who, way, h, arriving):
        sign = 1 if way == 0 else -1
        return wout.at[at_tp(-sign * (h + 1 if arriving else h)), weight_rows(who, way, h)]

    def weight_ring(way, h, arriving):
        sign = 1 if way == 0 else -1
        part = weight_part(dp, way, h, arriving)
        src = wo.at[weight_rows(dp, way, h)] if h == 0 and not arriving else part
        return remote(src, part, d_send.at[way, h], d_recv.at[way, h], {"tp": at_tp(sign)})

    def weight_beside(who, way, h):
        part = weight_part(who, way, h, True)
        return remote(part, part, x_send.at[way, h], x_recv.at[way, h], {"dp": beside})

    def weight_core(who, way, h, second):
        part = weight_part(who, way, h, True)
        sems = (f_send, f_recv) if second else (e_send, e_recv)
        return remote(part, part, sems[0].at[way, h], sems[1].at[way, h], {"dp": other_core})

    def exchange(c, r):
        return remote(outgoing.at[c, r], mixed.at[c, t], c_send.at[c, r], c_recv.at[c, r], {"tp": at_tp(r)})

    def exchange_arriving(c, r):
        part = mixed.at[c, at_tp(-r)]
        return remote(part, part, c_send.at[c, r], c_recv.at[c, r], {"tp": at_tp(r)})

    late = []

    def flush():
        while late:
            start(late.pop(0))

    def attend(c, g):
        if g == 0:
            blocks = [(t, None)]
        elif g == n_tp // 2:
            blocks = [(at_tp(g), g)]
        else:
            blocks = [(at_tp(-g), n_tp - g), (at_tp(g), g)]
        gain = g1[...]
        for i, (block, _) in enumerate(blocks):
            row = x_rows = xg[block, c * rows:(c + 1) * rows].astype(jnp.float32)
            scale = lax.rsqrt(jnp.mean(row * row, -1, keepdims=True) + EPSILON)
            normed[i * rows:(i + 1) * rows] = (x_rows * scale * gain).astype(jnp.bfloat16)
        total = len(blocks) * rows
        projected = jnp.dot(normed[:total], wqkv[...], preferred_element_type=jnp.float32)
        cos_part = cs[c * rows:(c + 1) * rows]
        sin_part = sn[c * rows:(c + 1) * rows]

        def rotate(part):
            return (part * cos_part + pltpu.roll(part, HEAD_WIDTH // 2, 1) * sin_part).astype(jnp.bfloat16)

        heads = group // HEAD_WIDTH
        query_at = lax.broadcasted_iota(jnp.int32, (heads * rows, seq), 0) % rows + c * rows
        key_at = lax.broadcasted_iota(jnp.int32, (heads * rows, seq), 1)
        for i, (block, r) in enumerate(blocks):
            part = projected[i * rows:(i + 1) * rows]
            query = jnp.concatenate(
                [rotate(part[:, h * HEAD_WIDTH:(h + 1) * HEAD_WIDTH]) for h in range(heads)], 0
            )
            keys[block, c * rows:(c + 1) * rows] = rotate(part[:, group:group + kv])
            values[block, c * rows:(c + 1) * rows] = part[:, group + kv:].astype(jnp.bfloat16)
            scores = lax.dot_general(
                query, keys[block], (((1,), (1,)), ((), ())), preferred_element_type=jnp.float32
            )
            capped = SOFT_CAP * jnp.tanh(scores * (QUERY_SCALE / SOFT_CAP))
            allowed = (key_at <= query_at) & (key_at < lens[0, block])
            raised = jnp.where(allowed, jnp.exp(capped), 0.0)
            probs = (raised / jnp.sum(raised, -1, keepdims=True)).astype(jnp.bfloat16)
            out = jnp.dot(probs, values[block], preferred_element_type=jnp.float32).astype(jnp.bfloat16)
            for h in range(heads):
                piece = out[h * rows:(h + 1) * rows]
                if r is None:
                    mixed[c, t, :, h * HEAD_WIDTH:(h + 1) * HEAD_WIDTH] = piece
                else:
                    outgoing[c, r, :, h * HEAD_WIDTH:(h + 1) * HEAD_WIDTH] = piece
            if r is not None:
                late.append(exchange(c, r))

    def finish(c):
        for r in range(1, n_tp):
            exchange_arriving(c, r).wait_recv()
        tile = 256
        square = jnp.zeros((rows, 1), jnp.float32)
        for n in range(width // tile):
            cols = slice(n * tile, (n + 1) * tile)
            acc = jnp.zeros((rows, tile), jnp.float32)
            for j in range(n_tp):
                acc += jnp.dot(mixed[c, j], wout[j, :, cols], preferred_element_type=jnp.float32)
            branch[:, cols] = acc
            square += jnp.sum(acc * acc, -1, keepdims=True)
        scale = lax.rsqrt(square / width + EPSILON)
        part = slice(c * rows, (c + 1) * rows)
        held = xg[t, part].astype(jnp.float32)
        made[part] = (held + branch[...] * scale * g2[...]).astype(jnp.bfloat16)
        copy = pltpu.make_async_copy(made.at[part], produced.at[part], o_sem.at[c])
        copy.start()

        @pl.when(section < n_section - 1)
        def _():
            send_on(c).start()

    def send_on(c):
        part = slice(c * rows, (c + 1) * rows)
        return remote(made.at[part], received.at[part], z_send.at[c], z_recv.at[c], {"section": section + 1})

    ready = False
    for step in STEPS:
        kind = step[0]
        if kind == "A":
            _, c, h = step
            for way in (0, 1):
                if h > 0:
                    ring(way, c, h - 1, True).wait_recv()
                if h < 4:
                    start(ring(way, c, h, False))
            flush()
        elif kind == "D":
            h = step[1]
            for way in (0, 1):
                if h > 0:
                    weight_ring(way, h - 1, True).wait_recv()
                if h < 4:
                    start(weight_ring(way, h, False))
                if h > 0:
                    start(weight_beside(dp, way, h - 1))
                    start(weight_core(dp, way, h - 1, False))
            flush()
        elif kind == "X":
            h = step[1]
            for way in (0, 1):
                weight_beside(beside, way, h).wait_recv()
                start(weight_core(beside, way, h, True))
            flush()
        elif kind == "W":
            for h in range(4):
                for way in (0, 1):
                    weight_core(other_core, way, h, False).wait_recv()
                    weight_core(lax.rem(other_core + 2, 4), way, h, True).wait_recv()
        elif kind == "U":
            if not ready:
                keys[...] = jnp.zeros_like(keys)
                values[...] = jnp.zeros_like(values)
                for copy in local:
                    copy.wait()
                ready = True
            flush()
            attend(step[1], step[2])
        else:
            flush()
            finish(step[1])

    for copy in pending:
        copy.wait_send()
    for c in range(CHUNKS):
        part = slice(c * rows, (c + 1) * rows)
        pltpu.make_async_copy(made.at[part], produced.at[part], o_sem.at[c]).wait()

    @pl.when(section < n_section - 1)
    def _():
        for c in range(CHUNKS):
            send_on(c).wait_send()

    @pl.when(section > 0)
    def _():
        for c in range(CHUNKS):
            send_on(c).wait_recv()


def tables(seq):
    half = HEAD_WIDTH // 2
    freq = 10000.0 ** (-2.0 * np.arange(half) / HEAD_WIDTH)
    angle = np.arange(seq)[:, None] * freq[None, :]
    cosine, sine = np.cos(angle), np.sin(angle)
    return (
        np.concatenate([cosine, cosine], -1).astype(np.float32),
        np.concatenate([-sine, sine], -1).astype(np.float32),
    )


def shards(
    n_section, n_tp, incoming, fresh_rows, entry_order, flight_lengths, pre_gain, post_gain,
    w_query, key_weight, value_weight, w_out,
):
    held = incoming[0, 0]
    seq, width = held.shape
    rows = seq // CHUNKS
    wq, wk, wv, wo = w_query[0], key_weight[0], value_weight[0], w_out[0]
    group, kv = wq.shape[1], wk.shape[1]
    cosine, sine = tables(seq)
    hbm = pl.BlockSpec(memory_space=pl.ANY)
    bf16, f32 = jnp.bfloat16, jnp.float32
    dma = pltpu.SemaphoreType.DMA
    produced, received = pl.pallas_call(
        functools.partial(kernel, n_section),
        out_shape=[jax.ShapeDtypeStruct((seq, width), bf16)] * 2,
        in_specs=[pl.BlockSpec(memory_space=pltpu.SMEM)] + [hbm] * 9,
        out_specs=[hbm] * 2,
        scratch_shapes=[
            pltpu.VMEM((n_tp, seq, width), bf16),
            pltpu.VMEM((width, group + 2 * kv), bf16),
            pltpu.VMEM((n_tp, group, width), bf16),
            pltpu.VMEM((n_tp, seq, kv), bf16),
            pltpu.VMEM((n_tp, seq, kv), bf16),
            pltpu.VMEM((2 * rows, width), bf16),
            pltpu.VMEM((CHUNKS, n_tp, rows, group), bf16),
            pltpu.VMEM((CHUNKS, n_tp, rows, group), bf16),
            pltpu.VMEM((rows, width), f32),
            pltpu.VMEM((seq, width), bf16),
            pltpu.VMEM((1, width), f32),
            pltpu.VMEM((1, width), f32),
            pltpu.VMEM((seq, HEAD_WIDTH), f32),
            pltpu.VMEM((seq, HEAD_WIDTH), f32),
            dma((2, CHUNKS, 4)), dma((2, CHUNKS, 4)),
            dma((2, 4)), dma((2, 4)), dma((2, 4)), dma((2, 4)), dma((2, 4)), dma((2, 4)), dma((2, 4)), dma((2, 4)),
            dma((CHUNKS, n_tp)), dma((CHUNKS, n_tp)),
            dma((CHUNKS,)), dma((CHUNKS,)), dma((9,)), dma((CHUNKS,)),
        ],
        compiler_params=pltpu.CompilerParams(
            collective_id=0, has_side_effects=True, vmem_limit_bytes=40 * 1024 * 1024
        ),
        name="relay",
    )(
        flight_lengths, held, pre_gain, post_gain, jnp.asarray(cosine), jnp.asarray(sine), wq, wk, wv, wo,
    )
    entering = lax.dynamic_index_in_dim(fresh_rows, entry_order[0], 0, keepdims=False)[0]
    advanced = jnp.where(lax.axis_index("section") == 0, entering, received)
    return produced[None, None], advanced[None, None]


def solution(mesh):
    in_specs = (
        P("section", ("dp", "tp"), None, None),
        P(None, ("dp", "tp"), None, None),
        P("dp"),
        P("section", "dp"),
        P("section", None),
        P("section", None),
        P("section", None, "tp"),
        P("section", None, "tp"),
        P("section", None, "tp"),
        P("section", "tp", None),
    )
    out_specs = (P("section", ("dp", "tp"), None, None), P("section", ("dp", "tp"), None, None))
    return jax.shard_map(
        functools.partial(shards, mesh.shape["section"], mesh.shape["tp"]),
        mesh=mesh, in_specs=in_specs, out_specs=out_specs, check_vma=False,
    )
```

```python
import functools

import jax
import jax.numpy as jnp
import numpy as np
from jax import lax
from jax.experimental import pallas as pl
from jax.experimental.pallas import tpu as pltpu
from jax.sharding import PartitionSpec as P

HEAD_WIDTH = 128
EPSILON = 1e-06
SOFT_CAP = 50.0
QUERY_SCALE = 144.0 ** (-0.5)
MESH = pl.DeviceIdType.MESH
SIZES = (64, 32, 16, 16)
CHUNKS = len(SIZES)
STARTS = [sum(SIZES[:c]) for c in range(CHUNKS)]

STEPS = [
    ("D", 0), ("A", 0, 0), ("D", 1), ("U", 0, 0), ("A", 0, 1), ("U", 1, 0), ("D", 2), ("X", 0), ("U", 2, 0),
    ("A", 0, 2), ("D", 3), ("A", 1, 0), ("X", 1), ("U", 0, 2), ("U", 0, 1), ("U", 3, 0), ("D", 4), ("A", 0, 3),
    ("A", 1, 1), ("U", 0, 3), ("A", 0, 4), ("X", 2), ("U", 0, 4), ("A", 2, 0), ("X", 3), ("U", 1, 1),
    ("A", 1, 2), ("U", 1, 2), ("A", 3, 0), ("W",), ("A", 2, 1), ("O", 0), ("A", 1, 3), ("U", 1, 3), ("A", 3, 1),
    ("U", 2, 1), ("A", 2, 2), ("A", 1, 4), ("U", 1, 4), ("U", 3, 1), ("A", 3, 2), ("U", 2, 2), ("A", 2, 3),
    ("U", 2, 3), ("A", 3, 3), ("O", 1), ("A", 2, 4), ("U", 2, 4), ("U", 3, 3), ("A", 3, 4), ("U", 3, 4),
    ("U", 3, 2), ("O", 2), ("O", 3),
]


def kernel(
    n_section, lengths, order, fresh, x, gain_before, gain_after, cosine, sine, wq, wk, wv, wo,
    produced, received,
    lens, chosen, pool, entering, xg, wqkv, wout, keys, values, normed, outgoing, mixed, branch, made, g1, g2, cs, sn,
    a_send, a_recv, d_send, d_recv, x_send, x_recv, e_send, e_recv, f_send, f_recv, c_send, c_recv,
    z_send, z_recv, l_sem, o_sem, p_sem,
):
    n_tp = wout.shape[0]
    section = lax.axis_index("section")
    t = lax.axis_index("tp")
    dp = lax.axis_index("dp")
    seq, width = x.shape
    group = wo.shape[0]
    quarter = group // 4
    kv = wk.shape[1]
    other_core = dp + 1 - 2 * lax.rem(dp, 2)
    beside = lax.rem(dp + 2, 4)

    def at_tp(distance):
        return lax.rem(t + n_tp + distance, n_tp)

    sources = (x, wq, wk, wv, wo, gain_before, gain_after, cosine, sine, lengths)
    targets = (
        xg.at[t], wqkv.at[:, :group], wqkv.at[:, group:group + kv], wqkv.at[:, group + kv:], wout.at[t], g1, g2, cs, sn,
        lens,
    )
    local = [pltpu.make_async_copy(s, d, l_sem.at[i]) for i, (s, d) in enumerate(zip(sources, targets))]
    for copy in local:
        copy.start()

    load_pool = [
        pltpu.make_async_copy(fresh, pool, p_sem.at[0]), pltpu.make_async_copy(order, chosen, p_sem.at[1])
    ]
    enter = pltpu.make_async_copy(entering, received, p_sem.at[2])

    barrier = pltpu.get_barrier_semaphore()
    for distance in range(1, n_tp):
        pl.semaphore_signal(barrier, inc=1, device_id={"tp": at_tp(distance)}, device_id_type=MESH)
    pl.semaphore_signal(barrier, inc=1, device_id={"dp": other_core}, device_id_type=MESH)
    pl.semaphore_signal(barrier, inc=1, device_id={"dp": beside}, device_id_type=MESH)

    for distance in (1, n_section - 1):
        pl.semaphore_signal(
            barrier, inc=1, device_id={"section": lax.rem(section + distance, n_section)}, device_id_type=MESH
        )
    pl.semaphore_wait(barrier, n_tp + 3)

    pending = []

    def remote(src, dst, send, recv, device):
        return pltpu.make_async_remote_copy(
            src_ref=src, dst_ref=dst, send_sem=send, recv_sem=recv, device_id=device, device_id_type=MESH
        )

    def start(copy):
        copy.start()
        pending.append(copy)

    def part_of(c):
        return slice(STARTS[c], STARTS[c] + SIZES[c])

    def ring_part(way, c, h):
        half = width // 2
        return part_of(c), slice(0, width) if h < 3 else slice(way * half, (way + 1) * half)

    def ring(way, c, h, arriving):
        sign = 1 if way == 0 else -1
        block = at_tp(-sign * (h + 1 if arriving else h))
        part = xg.at[(block, *ring_part(way, c, h))]
        src = x.at[part_of(c)] if h == 0 and not arriving else part
        return remote(src, part, a_send.at[way, c, h], a_recv.at[way, c, h], {"tp": at_tp(sign)})

    def weight_rows(who, way, h):
        if h < 3:
            return pl.ds(who * quarter, quarter)
        return pl.ds(who * quarter + way * (quarter // 2), quarter // 2)

    def weight_part(who, way, h, arriving):
        sign = 1 if way == 0 else -1
        return wout.at[at_tp(-sign * (h + 1 if arriving else h)), weight_rows(who, way, h)]

    def weight_ring(way, h, arriving):
        sign = 1 if way == 0 else -1
        part = weight_part(dp, way, h, arriving)
        src = wo.at[weight_rows(dp, way, h)] if h == 0 and not arriving else part
        return remote(src, part, d_send.at[way, h], d_recv.at[way, h], {"tp": at_tp(sign)})

    def weight_beside(who, way, h):
        part = weight_part(who, way, h, True)
        return remote(part, part, x_send.at[way, h], x_recv.at[way, h], {"dp": beside})

    def weight_core(who, way, h, second):
        part = weight_part(who, way, h, True)
        sems = (f_send, f_recv) if second else (e_send, e_recv)
        return remote(part, part, sems[0].at[way, h], sems[1].at[way, h], {"dp": other_core})

    def exchange(c, r):
        return remote(outgoing.at[r, part_of(c)], mixed.at[t, part_of(c)], c_send.at[c, r], c_recv.at[c, r], {"tp": at_tp(r)})

    def exchange_arriving(c, r):
        part = mixed.at[at_tp(-r), part_of(c)]
        return remote(part, part, c_send.at[c, r], c_recv.at[c, r], {"tp": at_tp(r)})

    late = []

    def flush():
        while late:
            start(late.pop(0))

    def attend(c, g):
        rows, at = SIZES[c], part_of(c)
        if g == 0:
            blocks = [(t, None)]
        elif g == n_tp // 2:
            blocks = [(at_tp(g), g)]
        else:
            blocks = [(at_tp(-g), n_tp - g), (at_tp(g), g)]
        gain = g1[...]
        for i, (block, _) in enumerate(blocks):
            held = xg[block, at].astype(jnp.float32)
            scale = lax.rsqrt(jnp.mean(held * held, -1, keepdims=True) + EPSILON)
            normed[i * rows:(i + 1) * rows] = (held * scale * gain).astype(jnp.bfloat16)
        total = len(blocks) * rows
        projected = jnp.dot(normed[:total], wqkv[...], preferred_element_type=jnp.float32)
        cos_part = cs[at]
        sin_part = sn[at]

        def rotate(part):
            return (part * cos_part + pltpu.roll(part, HEAD_WIDTH // 2, 1) * sin_part).astype(jnp.bfloat16)

        heads = group // HEAD_WIDTH
        query_at = lax.broadcasted_iota(jnp.int32, (heads * rows, seq), 0) % rows + STARTS[c]
        key_at = lax.broadcasted_iota(jnp.int32, (heads * rows, seq), 1)
        for i, (block, r) in enumerate(blocks):
            part = projected[i * rows:(i + 1) * rows]
            query = jnp.concatenate(
                [rotate(part[:, h * HEAD_WIDTH:(h + 1) * HEAD_WIDTH]) for h in range(heads)], 0
            )
            keys[block, at] = rotate(part[:, group:group + kv])
            values[block, at] = part[:, group + kv:].astype(jnp.bfloat16)
            scores = lax.dot_general(
                query, keys[block], (((1,), (1,)), ((), ())), preferred_element_type=jnp.float32
            )
            capped = SOFT_CAP * jnp.tanh(scores * (QUERY_SCALE / SOFT_CAP))
            allowed = (key_at <= query_at) & (key_at < lens[0, block])
            raised = jnp.where(allowed, jnp.exp(capped), 0.0)
            probs = (raised / jnp.sum(raised, -1, keepdims=True)).astype(jnp.bfloat16)
            out = jnp.dot(probs, values[block], preferred_element_type=jnp.float32).astype(jnp.bfloat16)
            for h in range(heads):
                piece = out[h * rows:(h + 1) * rows]
                if r is None:
                    mixed[t, at, h * HEAD_WIDTH:(h + 1) * HEAD_WIDTH] = piece
                else:
                    outgoing[r, at, h * HEAD_WIDTH:(h + 1) * HEAD_WIDTH] = piece
            if r is not None:
                late.append(exchange(c, r))

    def finish(c):
        rows, part = SIZES[c], part_of(c)
        for r in range(1, n_tp):
            exchange_arriving(c, r).wait_recv()
        tile = 256
        square = jnp.zeros((rows, 1), jnp.float32)
        for n in range(width // tile):
            cols = slice(n * tile, (n + 1) * tile)
            acc = jnp.zeros((rows, tile), jnp.float32)
            for j in range(n_tp):
                acc += jnp.dot(mixed[j, part], wout[j, :, cols], preferred_element_type=jnp.float32)
            branch[:rows, cols] = acc
            square += jnp.sum(acc * acc, -1, keepdims=True)
        scale = lax.rsqrt(square / width + EPSILON)
        held = xg[t, part].astype(jnp.float32)
        made[part] = (held + branch[:rows] * scale * g2[...]).astype(jnp.bfloat16)
        copy = pltpu.make_async_copy(made.at[part], produced.at[part], o_sem.at[c])
        copy.start()

        @pl.when(section < n_section - 1)
        def _():
            send_on(c).start()

    def send_on(c):
        part = part_of(c)
        return remote(made.at[part], received.at[part], z_send.at[c], z_recv.at[c], {"section": section + 1})

    ready = False
    for step in STEPS:
        kind = step[0]
        if kind == "A":
            _, c, h = step
            for way in (0, 1):
                if h > 0:
                    ring(way, c, h - 1, True).wait_recv()
                if h < 4:
                    start(ring(way, c, h, False))
            flush()
        elif kind == "D":
            h = step[1]
            for way in (0, 1):
                if h > 0:
                    weight_ring(way, h - 1, True).wait_recv()
                if h < 4:
                    start(weight_ring(way, h, False))
                if h > 0:
                    start(weight_beside(dp, way, h - 1))
                    start(weight_core(dp, way, h - 1, False))
            flush()
        elif kind == "X":
            h = step[1]
            for way in (0, 1):
                weight_beside(beside, way, h).wait_recv()
                start(weight_core(beside, way, h, True))
            flush()
        elif kind == "W":
            @pl.when(section == 0)
            def _():
                for copy in load_pool:
                    copy.wait()
                entering[...] = pool[chosen[0]]
                enter.start()

            for h in range(4):
                for way in (0, 1):
                    weight_core(other_core, way, h, False).wait_recv()
                    weight_core(lax.rem(other_core + 2, 4), way, h, True).wait_recv()
        elif kind == "U":
            if not ready:
                keys[...] = jnp.zeros_like(keys)
                values[...] = jnp.zeros_like(values)
                for copy in local:
                    copy.wait()

                @pl.when(section == 0)
                def _():
                    for copy in load_pool:
                        copy.start()

                ready = True
            flush()
            attend(step[1], step[2])
        else:
            flush()
            finish(step[1])

    @pl.when(section == 0)
    def _():
        enter.wait()

    for copy in pending:
        copy.wait_send()
    for c in range(CHUNKS):
        part = part_of(c)
        pltpu.make_async_copy(made.at[part], produced.at[part], o_sem.at[c]).wait()

    @pl.when(section < n_section - 1)
    def _():
        for c in range(CHUNKS):
            send_on(c).wait_send()

    @pl.when(section > 0)
    def _():
        for c in range(CHUNKS):
            send_on(c).wait_recv()


def tables(seq):
    half = HEAD_WIDTH // 2
    freq = 10000.0 ** (-2.0 * np.arange(half) / HEAD_WIDTH)
    angle = np.arange(seq)[:, None] * freq[None, :]
    cosine, sine = np.cos(angle), np.sin(angle)
    return (
        np.concatenate([cosine, cosine], -1).astype(np.float32),
        np.concatenate([-sine, sine], -1).astype(np.float32),
    )


def shards(
    n_section, n_tp, incoming, fresh_rows, entry_order, flight_lengths, pre_gain, post_gain,
    w_query, key_weight, value_weight, w_out,
):
    held = incoming[0, 0]
    seq, width = held.shape
    wq, wk, wv, wo = w_query[0], key_weight[0], value_weight[0], w_out[0]
    group, kv = wq.shape[1], wk.shape[1]
    cosine, sine = tables(seq)
    hbm = pl.BlockSpec(memory_space=pl.ANY)
    bf16, f32 = jnp.bfloat16, jnp.float32
    dma = pltpu.SemaphoreType.DMA
    produced, received = pl.pallas_call(
        functools.partial(kernel, n_section),
        out_shape=[jax.ShapeDtypeStruct((seq, width), bf16)] * 2,
        in_specs=[hbm] * 12,
        out_specs=[hbm] * 2,
        scratch_shapes=[
            pltpu.SMEM(flight_lengths.shape, jnp.int32),
            pltpu.SMEM(entry_order.shape, jnp.int32),
            pltpu.VMEM((fresh_rows.shape[0], seq, width), bf16),
            pltpu.VMEM((seq, width), bf16),
            pltpu.VMEM((n_tp, seq, width), bf16),
            pltpu.VMEM((width, group + 2 * kv), bf16),
            pltpu.VMEM((n_tp, group, width), bf16),
            pltpu.VMEM((n_tp, seq, kv), bf16),
            pltpu.VMEM((n_tp, seq, kv), bf16),
            pltpu.VMEM((2 * max(SIZES), width), bf16),
            pltpu.VMEM((n_tp, seq, group), bf16),
            pltpu.VMEM((n_tp, seq, group), bf16),
            pltpu.VMEM((max(SIZES), width), f32),
            pltpu.VMEM((seq, width), bf16),
            pltpu.VMEM((1, width), f32),
            pltpu.VMEM((1, width), f32),
            pltpu.VMEM((seq, HEAD_WIDTH), f32),
            pltpu.VMEM((seq, HEAD_WIDTH), f32),
            dma((2, CHUNKS, 4)), dma((2, CHUNKS, 4)),
            dma((2, 4)), dma((2, 4)), dma((2, 4)), dma((2, 4)), dma((2, 4)), dma((2, 4)), dma((2, 4)), dma((2, 4)),
            dma((CHUNKS, n_tp)), dma((CHUNKS, n_tp)),
            dma((CHUNKS,)), dma((CHUNKS,)), dma((10,)), dma((CHUNKS,)), dma((3,)),
        ],
        compiler_params=pltpu.CompilerParams(
            collective_id=0, has_side_effects=True, vmem_limit_bytes=67043328
        ),
        name="relay",
    )(
        flight_lengths, entry_order, fresh_rows[:, 0], held, pre_gain, post_gain, jnp.asarray(cosine), jnp.asarray(sine), wq, wk, wv, wo,
    )
    return produced[None, None], received[None, None]


def solution(mesh):
    in_specs = (
        P("section", ("dp", "tp"), None, None),
        P(None, ("dp", "tp"), None, None),
        P("dp"),
        P("section", "dp"),
        P("section", None),
        P("section", None),
        P("section", None, "tp"),
        P("section", None, "tp"),
        P("section", None, "tp"),
        P("section", "tp", None),
    )
    out_specs = (P("section", ("dp", "tp"), None, None), P("section", ("dp", "tp"), None, None))
    return jax.shard_map(
        functools.partial(shards, mesh.shape["section"], mesh.shape["tp"]),
        mesh=mesh, in_specs=in_specs, out_specs=out_specs, check_vma=False,
    )
```

```python
import functools

import jax
import jax.numpy as jnp
import numpy as np
from jax import lax
from jax.experimental import pallas as pl
from jax.experimental.pallas import tpu as pltpu
from jax.sharding import PartitionSpec as P

HEAD_WIDTH = 128
EPSILON = 1e-06
SOFT_CAP = 50.0
QUERY_SCALE = 144.0 ** (-0.5)
MESH = pl.DeviceIdType.MESH
SIZES = (48, 32, 16, 16, 16)
CHUNKS = len(SIZES)
STARTS = [sum(SIZES[:c]) for c in range(CHUNKS)]

STEPS = [
    ("D", 0), ("A", 0, 0), ("D", 1), ("A", 0, 1), ("D", 2), ("X", 0), ("A", 1, 0), ("D", 3), ("A", 2, 0),
    ("A", 0, 2), ("U", 0, 0), ("U", 0, 2), ("A", 1, 1), ("X", 1), ("A", 3, 0), ("A", 0, 3), ("U", 1, 0),
    ("D", 4), ("A", 2, 1), ("A", 1, 2), ("X", 2), ("U", 2, 0), ("U", 0, 3), ("A", 0, 4), ("U", 3, 0),
    ("U", 0, 4), ("U", 0, 1), ("A", 4, 0), ("X", 3), ("A", 1, 3), ("A", 2, 2), ("W",), ("A", 4, 1), ("O", 0),
    ("A", 1, 4), ("A", 3, 1), ("U", 1, 3), ("U", 1, 4), ("U", 1, 2), ("A", 2, 3), ("U", 4, 0), ("U", 1, 1),
    ("A", 3, 2), ("A", 4, 2), ("U", 2, 2), ("U", 2, 3), ("A", 2, 4), ("U", 2, 4), ("O", 1), ("A", 3, 3),
    ("U", 2, 1), ("U", 3, 1), ("A", 4, 3), ("U", 3, 3), ("U", 4, 3), ("A", 3, 4), ("U", 3, 4), ("U", 3, 2),
    ("A", 4, 4), ("U", 4, 4), ("O", 2), ("U", 4, 2), ("U", 4, 1), ("O", 3), ("O", 4),
]


def kernel(
    n_section, lengths, order, fresh, x, gain_before, gain_after, cosine, sine, wq, wk, wv, wo,
    produced, received,
    lens, chosen, pool, entering, xg, wqkv, wout, keys, values, normed, outgoing, mixed, branch, made, g1, g2, cs, sn,
    a_send, a_recv, d_send, d_recv, x_send, x_recv, e_send, e_recv, f_send, f_recv, c_send, c_recv,
    z_send, z_recv, l_sem, o_sem, p_sem,
):
    n_tp = wout.shape[0]
    section = lax.axis_index("section")
    t = lax.axis_index("tp")
    dp = lax.axis_index("dp")
    seq, width = x.shape
    group = wo.shape[0]
    quarter = group // 4
    kv = wk.shape[1]
    other_core = dp + 1 - 2 * lax.rem(dp, 2)
    beside = lax.rem(dp + 2, 4)

    def at_tp(distance):
        return lax.rem(t + n_tp + distance, n_tp)

    sources = (x, wq, wk, wv, wo, gain_before, gain_after, cosine, sine, lengths)
    targets = (
        xg.at[t], wqkv.at[:, :group], wqkv.at[:, group:group + kv], wqkv.at[:, group + kv:], wout.at[t], g1, g2, cs, sn,
        lens,
    )
    local = [pltpu.make_async_copy(s, d, l_sem.at[i]) for i, (s, d) in enumerate(zip(sources, targets))]
    for copy in local:
        copy.start()

    load_pool = [
        pltpu.make_async_copy(fresh, pool, p_sem.at[0]), pltpu.make_async_copy(order, chosen, p_sem.at[1])
    ]
    enter = pltpu.make_async_copy(entering, received, p_sem.at[2])

    barrier = pltpu.get_barrier_semaphore()
    for distance in range(1, n_tp):
        pl.semaphore_signal(barrier, inc=1, device_id={"tp": at_tp(distance)}, device_id_type=MESH)
    pl.semaphore_signal(barrier, inc=1, device_id={"dp": other_core}, device_id_type=MESH)
    pl.semaphore_signal(barrier, inc=1, device_id={"dp": beside}, device_id_type=MESH)

    for distance in (1, n_section - 1):
        pl.semaphore_signal(
            barrier, inc=1, device_id={"section": lax.rem(section + distance, n_section)}, device_id_type=MESH
        )
    pl.semaphore_wait(barrier, n_tp + 3)

    pending = []

    def remote(src, dst, send, recv, device):
        return pltpu.make_async_remote_copy(
            src_ref=src, dst_ref=dst, send_sem=send, recv_sem=recv, device_id=device, device_id_type=MESH
        )

    def start(copy):
        copy.start()
        pending.append(copy)

    def part_of(c):
        return slice(STARTS[c], STARTS[c] + SIZES[c])

    def ring_part(way, c, h):
        half = width // 2
        return part_of(c), slice(0, width) if h < 3 else slice(way * half, (way + 1) * half)

    def ring(way, c, h, arriving):
        sign = 1 if way == 0 else -1
        block = at_tp(-sign * (h + 1 if arriving else h))
        part = xg.at[(block, *ring_part(way, c, h))]
        src = x.at[part_of(c)] if h == 0 and not arriving else part
        return remote(src, part, a_send.at[way, c, h], a_recv.at[way, c, h], {"tp": at_tp(sign)})

    def weight_rows(who, way, h):
        if h < 3:
            return pl.ds(who * quarter, quarter)
        return pl.ds(who * quarter + way * (quarter // 2), quarter // 2)

    def weight_part(who, way, h, arriving):
        sign = 1 if way == 0 else -1
        return wout.at[at_tp(-sign * (h + 1 if arriving else h)), weight_rows(who, way, h)]

    def weight_ring(way, h, arriving):
        sign = 1 if way == 0 else -1
        part = weight_part(dp, way, h, arriving)
        src = wo.at[weight_rows(dp, way, h)] if h == 0 and not arriving else part
        return remote(src, part, d_send.at[way, h], d_recv.at[way, h], {"tp": at_tp(sign)})

    def weight_beside(who, way, h):
        part = weight_part(who, way, h, True)
        return remote(part, part, x_send.at[way, h], x_recv.at[way, h], {"dp": beside})

    def weight_core(who, way, h, second):
        part = weight_part(who, way, h, True)
        sems = (f_send, f_recv) if second else (e_send, e_recv)
        return remote(part, part, sems[0].at[way, h], sems[1].at[way, h], {"dp": other_core})

    def exchange(c, r):
        return remote(outgoing.at[r, part_of(c)], mixed.at[t, part_of(c)], c_send.at[c, r], c_recv.at[c, r], {"tp": at_tp(r)})

    def exchange_arriving(c, r):
        part = mixed.at[at_tp(-r), part_of(c)]
        return remote(part, part, c_send.at[c, r], c_recv.at[c, r], {"tp": at_tp(r)})

    late = []

    def flush():
        while late:
            start(late.pop(0))

    def attend(c, g):
        rows, at = SIZES[c], part_of(c)
        if g == 0:
            blocks = [(t, None)]
        elif g == n_tp // 2:
            blocks = [(at_tp(g), g)]
        else:
            blocks = [(at_tp(-g), n_tp - g), (at_tp(g), g)]
        gain = g1[...]
        for i, (block, _) in enumerate(blocks):
            held = xg[block, at].astype(jnp.float32)
            scale = lax.rsqrt(jnp.mean(held * held, -1, keepdims=True) + EPSILON)
            normed[i * rows:(i + 1) * rows] = (held * scale * gain).astype(jnp.bfloat16)
        total = len(blocks) * rows
        projected = jnp.dot(normed[:total], wqkv[...], preferred_element_type=jnp.float32)
        cos_part = cs[at]
        sin_part = sn[at]

        def rotate(part):
            return (part * cos_part + pltpu.roll(part, HEAD_WIDTH // 2, 1) * sin_part).astype(jnp.bfloat16)

        heads = group // HEAD_WIDTH
        query_at = lax.broadcasted_iota(jnp.int32, (heads * rows, seq), 0) % rows + STARTS[c]
        key_at = lax.broadcasted_iota(jnp.int32, (heads * rows, seq), 1)
        for i, (block, r) in enumerate(blocks):
            part = projected[i * rows:(i + 1) * rows]
            query = jnp.concatenate(
                [rotate(part[:, h * HEAD_WIDTH:(h + 1) * HEAD_WIDTH]) for h in range(heads)], 0
            )
            keys[block, at] = rotate(part[:, group:group + kv])
            values[block, at] = part[:, group + kv:].astype(jnp.bfloat16)
            scores = lax.dot_general(
                query, keys[block], (((1,), (1,)), ((), ())), preferred_element_type=jnp.float32
            )
            capped = SOFT_CAP * jnp.tanh(scores * (QUERY_SCALE / SOFT_CAP))
            allowed = (key_at <= query_at) & (key_at < lens[0, block])
            raised = jnp.where(allowed, jnp.exp(capped), 0.0)
            probs = (raised / jnp.sum(raised, -1, keepdims=True)).astype(jnp.bfloat16)
            out = jnp.dot(probs, values[block], preferred_element_type=jnp.float32).astype(jnp.bfloat16)
            for h in range(heads):
                piece = out[h * rows:(h + 1) * rows]
                if r is None:
                    mixed[t, at, h * HEAD_WIDTH:(h + 1) * HEAD_WIDTH] = piece
                else:
                    outgoing[r, at, h * HEAD_WIDTH:(h + 1) * HEAD_WIDTH] = piece
            if r is not None:
                late.append(exchange(c, r))

    def finish(c):
        rows, part = SIZES[c], part_of(c)
        for r in range(1, n_tp):
            exchange_arriving(c, r).wait_recv()
        tile = 256
        square = jnp.zeros((rows, 1), jnp.float32)
        for n in range(width // tile):
            cols = slice(n * tile, (n + 1) * tile)
            acc = jnp.zeros((rows, tile), jnp.float32)
            for j in range(n_tp):
                acc += jnp.dot(mixed[j, part], wout[j, :, cols], preferred_element_type=jnp.float32)
            branch[:rows, cols] = acc
            square += jnp.sum(acc * acc, -1, keepdims=True)
        scale = lax.rsqrt(square / width + EPSILON)
        held = xg[t, part].astype(jnp.float32)
        made[part] = (held + branch[:rows] * scale * g2[...]).astype(jnp.bfloat16)
        copy = pltpu.make_async_copy(made.at[part], produced.at[part], o_sem.at[c])
        copy.start()

        @pl.when(section < n_section - 1)
        def _():
            send_on(c).start()

    def send_on(c):
        part = part_of(c)
        return remote(made.at[part], received.at[part], z_send.at[c], z_recv.at[c], {"section": section + 1})

    ready = False
    for step in STEPS:
        kind = step[0]
        if kind == "A":
            _, c, h = step
            for way in (0, 1):
                if h > 0:
                    ring(way, c, h - 1, True).wait_recv()
                if h < 4:
                    start(ring(way, c, h, False))
            flush()
        elif kind == "D":
            h = step[1]
            for way in (0, 1):
                if h > 0:
                    weight_ring(way, h - 1, True).wait_recv()
                if h < 4:
                    start(weight_ring(way, h, False))
                if h > 0:
                    start(weight_beside(dp, way, h - 1))
                    start(weight_core(dp, way, h - 1, False))
            flush()
        elif kind == "X":
            h = step[1]
            for way in (0, 1):
                weight_beside(beside, way, h).wait_recv()
                start(weight_core(beside, way, h, True))
            flush()
        elif kind == "W":
            @pl.when(section == 0)
            def _():
                for copy in load_pool:
                    copy.wait()
                entering[...] = pool[chosen[0]]
                enter.start()

            for h in range(4):
                for way in (0, 1):
                    weight_core(other_core, way, h, False).wait_recv()
                    weight_core(lax.rem(other_core + 2, 4), way, h, True).wait_recv()
        elif kind == "U":
            if not ready:
                keys[...] = jnp.zeros_like(keys)
                values[...] = jnp.zeros_like(values)
                for copy in local:
                    copy.wait()

                @pl.when(section == 0)
                def _():
                    for copy in load_pool:
                        copy.start()

                ready = True
            flush()
            attend(step[1], step[2])
        else:
            flush()
            finish(step[1])

    @pl.when(section == 0)
    def _():
        enter.wait()

    for copy in pending:
        copy.wait_send()
    for c in range(CHUNKS):
        part = part_of(c)
        pltpu.make_async_copy(made.at[part], produced.at[part], o_sem.at[c]).wait()

    @pl.when(section < n_section - 1)
    def _():
        for c in range(CHUNKS):
            send_on(c).wait_send()

    @pl.when(section > 0)
    def _():
        for c in range(CHUNKS):
            send_on(c).wait_recv()


def tables(seq):
    half = HEAD_WIDTH // 2
    freq = 10000.0 ** (-2.0 * np.arange(half) / HEAD_WIDTH)
    angle = np.arange(seq)[:, None] * freq[None, :]
    cosine, sine = np.cos(angle), np.sin(angle)
    return (
        np.concatenate([cosine, cosine], -1).astype(np.float32),
        np.concatenate([-sine, sine], -1).astype(np.float32),
    )


def shards(
    n_section, n_tp, incoming, fresh_rows, entry_order, flight_lengths, pre_gain, post_gain,
    w_query, key_weight, value_weight, w_out,
):
    held = incoming[0, 0]
    seq, width = held.shape
    wq, wk, wv, wo = w_query[0], key_weight[0], value_weight[0], w_out[0]
    group, kv = wq.shape[1], wk.shape[1]
    cosine, sine = tables(seq)
    hbm = pl.BlockSpec(memory_space=pl.ANY)
    bf16, f32 = jnp.bfloat16, jnp.float32
    dma = pltpu.SemaphoreType.DMA
    produced, received = pl.pallas_call(
        functools.partial(kernel, n_section),
        out_shape=[jax.ShapeDtypeStruct((seq, width), bf16)] * 2,
        in_specs=[hbm] * 12,
        out_specs=[hbm] * 2,
        scratch_shapes=[
            pltpu.SMEM(flight_lengths.shape, jnp.int32),
            pltpu.SMEM(entry_order.shape, jnp.int32),
            pltpu.VMEM((fresh_rows.shape[0], seq, width), bf16),
            pltpu.VMEM((seq, width), bf16),
            pltpu.VMEM((n_tp, seq, width), bf16),
            pltpu.VMEM((width, group + 2 * kv), bf16),
            pltpu.VMEM((n_tp, group, width), bf16),
            pltpu.VMEM((n_tp, seq, kv), bf16),
            pltpu.VMEM((n_tp, seq, kv), bf16),
            pltpu.VMEM((2 * max(SIZES), width), bf16),
            pltpu.VMEM((n_tp, seq, group), bf16),
            pltpu.VMEM((n_tp, seq, group), bf16),
            pltpu.VMEM((max(SIZES), width), f32),
            pltpu.VMEM((seq, width), bf16),
            pltpu.VMEM((1, width), f32),
            pltpu.VMEM((1, width), f32),
            pltpu.VMEM((seq, HEAD_WIDTH), f32),
            pltpu.VMEM((seq, HEAD_WIDTH), f32),
            dma((2, CHUNKS, 4)), dma((2, CHUNKS, 4)),
            dma((2, 4)), dma((2, 4)), dma((2, 4)), dma((2, 4)), dma((2, 4)), dma((2, 4)), dma((2, 4)), dma((2, 4)),
            dma((CHUNKS, n_tp)), dma((CHUNKS, n_tp)),
            dma((CHUNKS,)), dma((CHUNKS,)), dma((10,)), dma((CHUNKS,)), dma((3,)),
        ],
        compiler_params=pltpu.CompilerParams(
            collective_id=0, has_side_effects=True, vmem_limit_bytes=67043328
        ),
        name="relay",
    )(
        flight_lengths, entry_order, fresh_rows[:, 0], held, pre_gain, post_gain, jnp.asarray(cosine), jnp.asarray(sine), wq, wk, wv, wo,
    )
    return produced[None, None], received[None, None]


def solution(mesh):
    in_specs = (
        P("section", ("dp", "tp"), None, None),
        P(None, ("dp", "tp"), None, None),
        P("dp"),
        P("section", "dp"),
        P("section", None),
        P("section", None),
        P("section", None, "tp"),
        P("section", None, "tp"),
        P("section", None, "tp"),
        P("section", "tp", None),
    )
    out_specs = (P("section", ("dp", "tp"), None, None), P("section", ("dp", "tp"), None, None))
    return jax.shard_map(
        functools.partial(shards, mesh.shape["section"], mesh.shape["tp"]),
        mesh=mesh, in_specs=in_specs, out_specs=out_specs, check_vma=False,
    )
```

```python
import functools

import jax
import jax.numpy as jnp
import numpy as np
from jax import lax
from jax.experimental import pallas as pl
from jax.experimental.pallas import tpu as pltpu
from jax.sharding import PartitionSpec as P

HEAD_WIDTH = 128
EPSILON = 1e-06
SOFT_CAP = 50.0
QUERY_SCALE = 144.0 ** (-0.5)
MESH = pl.DeviceIdType.MESH
SIZES = (64, 48, 16)
CHUNKS = len(SIZES)
STARTS = [sum(SIZES[:c]) for c in range(CHUNKS)]

STEPS = [
    ("D", 0), ("U", 0, 0), ("U", 1, 0), ("A", 0, 0), ("D", 1), ("A", 0, 1), ("D", 2), ("X", 0), ("A", 0, 2),
    ("U", 0, 1), ("D", 3), ("U", 2, 0), ("X", 1), ("A", 1, 0), ("D", 4), ("A", 0, 3), ("U", 0, 3), ("A", 1, 1),
    ("X", 2), ("U", 0, 2), ("X", 3), ("A", 0, 4), ("U", 0, 4), ("A", 1, 2), ("A", 2, 0), ("W",), ("U", 1, 2),
    ("O", 0), ("A", 1, 3), ("A", 2, 1), ("U", 1, 3), ("A", 1, 4), ("U", 1, 4), ("A", 2, 2), ("U", 1, 1),
    ("U", 2, 2), ("A", 2, 3), ("O", 1), ("A", 2, 4), ("U", 2, 4), ("U", 2, 3), ("U", 2, 1), ("O", 2),
]


def kernel(
    n_section, lengths, order, fresh, x, gain_before, gain_after, cosine, sine, wq, wk, wv, wo,
    produced, received,
    lens, chosen, pool, entering, xg, wqkv, wout, keys, values, normed, outgoing, mixed, branch, made, g1, g2, cs, sn,
    a_send, a_recv, d_send, d_recv, x_send, x_recv, e_send, e_recv, f_send, f_recv, c_send, c_recv,
    z_send, z_recv, l_sem, o_sem, p_sem,
):
    n_tp = wout.shape[0]
    section = lax.axis_index("section")
    t = lax.axis_index("tp")
    dp = lax.axis_index("dp")
    seq, width = x.shape
    group = wo.shape[0]
    quarter = group // 4
    kv = wk.shape[1]
    other_core = dp + 1 - 2 * lax.rem(dp, 2)
    beside = lax.rem(dp + 2, 4)

    def at_tp(distance):
        return lax.rem(t + n_tp + distance, n_tp)

    sources = (x, wq, wk, wv, wo, gain_before, gain_after, cosine, sine, lengths)
    targets = (
        xg.at[t], wqkv.at[:, :group], wqkv.at[:, group:group + kv], wqkv.at[:, group + kv:], wout.at[t], g1, g2, cs, sn,
        lens,
    )
    local = [pltpu.make_async_copy(s, d, l_sem.at[i]) for i, (s, d) in enumerate(zip(sources, targets))]
    for copy in local:
        copy.start()

    load_pool = [
        pltpu.make_async_copy(fresh, pool, p_sem.at[0]), pltpu.make_async_copy(order, chosen, p_sem.at[1])
    ]
    enter = pltpu.make_async_copy(entering, received, p_sem.at[2])

    barrier = pltpu.get_barrier_semaphore()
    for distance in range(1, n_tp):
        pl.semaphore_signal(barrier, inc=1, device_id={"tp": at_tp(distance)}, device_id_type=MESH)
    pl.semaphore_signal(barrier, inc=1, device_id={"dp": other_core}, device_id_type=MESH)
    pl.semaphore_signal(barrier, inc=1, device_id={"dp": beside}, device_id_type=MESH)

    for distance in (1, n_section - 1):
        pl.semaphore_signal(
            barrier, inc=1, device_id={"section": lax.rem(section + distance, n_section)}, device_id_type=MESH
        )
    pl.semaphore_wait(barrier, n_tp + 3)

    pending = []

    def remote(src, dst, send, recv, device):
        return pltpu.make_async_remote_copy(
            src_ref=src, dst_ref=dst, send_sem=send, recv_sem=recv, device_id=device, device_id_type=MESH
        )

    def start(copy):
        copy.start()
        pending.append(copy)

    def part_of(c):
        return slice(STARTS[c], STARTS[c] + SIZES[c])

    def ring_part(way, c, h):
        half = width // 2
        return part_of(c), slice(0, width) if h < 3 else slice(way * half, (way + 1) * half)

    def ring(way, c, h, arriving):
        sign = 1 if way == 0 else -1
        block = at_tp(-sign * (h + 1 if arriving else h))
        part = xg.at[(block, *ring_part(way, c, h))]
        src = x.at[part_of(c)] if h == 0 and not arriving else part
        return remote(src, part, a_send.at[way, c, h], a_recv.at[way, c, h], {"tp": at_tp(sign)})

    def weight_rows(who, way, h):
        if h < 3:
            return pl.ds(who * quarter, quarter)
        return pl.ds(who * quarter + way * (quarter // 2), quarter // 2)

    def weight_part(who, way, h, arriving):
        sign = 1 if way == 0 else -1
        return wout.at[at_tp(-sign * (h + 1 if arriving else h)), weight_rows(who, way, h)]

    def weight_ring(way, h, arriving):
        sign = 1 if way == 0 else -1
        part = weight_part(dp, way, h, arriving)
        src = wo.at[weight_rows(dp, way, h)] if h == 0 and not arriving else part
        return remote(src, part, d_send.at[way, h], d_recv.at[way, h], {"tp": at_tp(sign)})

    def weight_beside(who, way, h):
        part = weight_part(who, way, h, True)
        return remote(part, part, x_send.at[way, h], x_recv.at[way, h], {"dp": beside})

    def weight_core(who, way, h, second):
        part = weight_part(who, way, h, True)
        sems = (f_send, f_recv) if second else (e_send, e_recv)
        return remote(part, part, sems[0].at[way, h], sems[1].at[way, h], {"dp": other_core})

    def exchange(c, r):
        return remote(outgoing.at[r, part_of(c)], mixed.at[t, part_of(c)], c_send.at[c, r], c_recv.at[c, r], {"tp": at_tp(r)})

    def exchange_arriving(c, r):
        part = mixed.at[at_tp(-r), part_of(c)]
        return remote(part, part, c_send.at[c, r], c_recv.at[c, r], {"tp": at_tp(r)})

    late = []

    def flush():
        while late:
            start(late.pop(0))

    def attend(c, g):
        rows, at = SIZES[c], part_of(c)
        if g == 0:
            blocks = [(t, None)]
        elif g == n_tp // 2:
            blocks = [(at_tp(g), g)]
        else:
            blocks = [(at_tp(-g), n_tp - g), (at_tp(g), g)]
        gain = g1[...]
        for i, (block, _) in enumerate(blocks):
            held = xg[block, at].astype(jnp.float32)
            scale = lax.rsqrt(jnp.mean(held * held, -1, keepdims=True) + EPSILON)
            normed[i * rows:(i + 1) * rows] = (held * scale * gain).astype(jnp.bfloat16)
        total = len(blocks) * rows
        projected = jnp.dot(normed[:total], wqkv[...], preferred_element_type=jnp.float32)
        cos_part = cs[at]
        sin_part = sn[at]

        def rotate(part):
            return (part * cos_part + pltpu.roll(part, HEAD_WIDTH // 2, 1) * sin_part).astype(jnp.bfloat16)

        heads = group // HEAD_WIDTH
        query_at = lax.broadcasted_iota(jnp.int32, (heads * rows, seq), 0) % rows + STARTS[c]
        key_at = lax.broadcasted_iota(jnp.int32, (heads * rows, seq), 1)
        for i, (block, r) in enumerate(blocks):
            part = projected[i * rows:(i + 1) * rows]
            query = jnp.concatenate(
                [rotate(part[:, h * HEAD_WIDTH:(h + 1) * HEAD_WIDTH]) for h in range(heads)], 0
            )
            keys[block, at] = rotate(part[:, group:group + kv])
            values[block, at] = part[:, group + kv:].astype(jnp.bfloat16)
            scores = lax.dot_general(
                query, keys[block], (((1,), (1,)), ((), ())), preferred_element_type=jnp.float32
            )
            capped = SOFT_CAP * jnp.tanh(scores * (QUERY_SCALE / SOFT_CAP))
            allowed = (key_at <= query_at) & (key_at < lens[0, block])
            raised = jnp.where(allowed, jnp.exp(capped), 0.0)
            probs = (raised / jnp.sum(raised, -1, keepdims=True)).astype(jnp.bfloat16)
            out = jnp.dot(probs, values[block], preferred_element_type=jnp.float32).astype(jnp.bfloat16)
            for h in range(heads):
                piece = out[h * rows:(h + 1) * rows]
                if r is None:
                    mixed[t, at, h * HEAD_WIDTH:(h + 1) * HEAD_WIDTH] = piece
                else:
                    outgoing[r, at, h * HEAD_WIDTH:(h + 1) * HEAD_WIDTH] = piece
            if r is not None:
                late.append(exchange(c, r))

    def finish(c):
        rows, part = SIZES[c], part_of(c)
        for r in range(1, n_tp):
            exchange_arriving(c, r).wait_recv()
        tile = 256
        square = jnp.zeros((rows, 1), jnp.float32)
        for n in range(width // tile):
            cols = slice(n * tile, (n + 1) * tile)
            acc = jnp.zeros((rows, tile), jnp.float32)
            for j in range(n_tp):
                acc += jnp.dot(mixed[j, part], wout[j, :, cols], preferred_element_type=jnp.float32)
            branch[:rows, cols] = acc
            square += jnp.sum(acc * acc, -1, keepdims=True)
        scale = lax.rsqrt(square / width + EPSILON)
        held = xg[t, part].astype(jnp.float32)
        made[part] = (held + branch[:rows] * scale * g2[...]).astype(jnp.bfloat16)
        copy = pltpu.make_async_copy(made.at[part], produced.at[part], o_sem.at[c])
        copy.start()

        @pl.when(section < n_section - 1)
        def _():
            send_on(c).start()

    def send_on(c):
        part = part_of(c)
        return remote(made.at[part], received.at[part], z_send.at[c], z_recv.at[c], {"section": section + 1})

    ready = False
    for step in STEPS:
        kind = step[0]
        if kind == "A":
            _, c, h = step
            for way in (0, 1):
                if h > 0:
                    ring(way, c, h - 1, True).wait_recv()
                if h < 4:
                    start(ring(way, c, h, False))
            flush()
        elif kind == "D":
            h = step[1]
            for way in (0, 1):
                if h > 0:
                    weight_ring(way, h - 1, True).wait_recv()
                if h < 4:
                    start(weight_ring(way, h, False))
                if h > 0:
                    start(weight_beside(dp, way, h - 1))
                    start(weight_core(dp, way, h - 1, False))
            flush()
        elif kind == "X":
            h = step[1]
            for way in (0, 1):
                weight_beside(beside, way, h).wait_recv()
                start(weight_core(beside, way, h, True))
            flush()
        elif kind == "W":
            @pl.when(section == 0)
            def _():
                for copy in load_pool:
                    copy.wait()
                entering[...] = pool[chosen[0]]
                enter.start()

            for h in range(4):
                for way in (0, 1):
                    weight_core(other_core, way, h, False).wait_recv()
                    weight_core(lax.rem(other_core + 2, 4), way, h, True).wait_recv()
        elif kind == "U":
            if not ready:
                keys[...] = jnp.zeros_like(keys)
                values[...] = jnp.zeros_like(values)
                for copy in local:
                    copy.wait()

                @pl.when(section == 0)
                def _():
                    for copy in load_pool:
                        copy.start()

                ready = True
            flush()
            attend(step[1], step[2])
        else:
            flush()
            finish(step[1])

    @pl.when(section == 0)
    def _():
        enter.wait()

    for copy in pending:
        copy.wait_send()
    for c in range(CHUNKS):
        part = part_of(c)
        pltpu.make_async_copy(made.at[part], produced.at[part], o_sem.at[c]).wait()

    @pl.when(section < n_section - 1)
    def _():
        for c in range(CHUNKS):
            send_on(c).wait_send()

    @pl.when(section > 0)
    def _():
        for c in range(CHUNKS):
            send_on(c).wait_recv()


def tables(seq):
    half = HEAD_WIDTH // 2
    freq = 10000.0 ** (-2.0 * np.arange(half) / HEAD_WIDTH)
    angle = np.arange(seq)[:, None] * freq[None, :]
    cosine, sine = np.cos(angle), np.sin(angle)
    return (
        np.concatenate([cosine, cosine], -1).astype(np.float32),
        np.concatenate([-sine, sine], -1).astype(np.float32),
    )


def shards(
    n_section, n_tp, incoming, fresh_rows, entry_order, flight_lengths, pre_gain, post_gain,
    w_query, key_weight, value_weight, w_out,
):
    held = incoming[0, 0]
    seq, width = held.shape
    wq, wk, wv, wo = w_query[0], key_weight[0], value_weight[0], w_out[0]
    group, kv = wq.shape[1], wk.shape[1]
    cosine, sine = tables(seq)
    hbm = pl.BlockSpec(memory_space=pl.ANY)
    bf16, f32 = jnp.bfloat16, jnp.float32
    dma = pltpu.SemaphoreType.DMA
    produced, received = pl.pallas_call(
        functools.partial(kernel, n_section),
        out_shape=[jax.ShapeDtypeStruct((seq, width), bf16)] * 2,
        in_specs=[hbm] * 12,
        out_specs=[hbm] * 2,
        scratch_shapes=[
            pltpu.SMEM(flight_lengths.shape, jnp.int32),
            pltpu.SMEM(entry_order.shape, jnp.int32),
            pltpu.VMEM((fresh_rows.shape[0], seq, width), bf16),
            pltpu.VMEM((seq, width), bf16),
            pltpu.VMEM((n_tp, seq, width), bf16),
            pltpu.VMEM((width, group + 2 * kv), bf16),
            pltpu.VMEM((n_tp, group, width), bf16),
            pltpu.VMEM((n_tp, seq, kv), bf16),
            pltpu.VMEM((n_tp, seq, kv), bf16),
            pltpu.VMEM((2 * max(SIZES), width), bf16),
            pltpu.VMEM((n_tp, seq, group), bf16),
            pltpu.VMEM((n_tp, seq, group), bf16),
            pltpu.VMEM((max(SIZES), width), f32),
            pltpu.VMEM((seq, width), bf16),
            pltpu.VMEM((1, width), f32),
            pltpu.VMEM((1, width), f32),
            pltpu.VMEM((seq, HEAD_WIDTH), f32),
            pltpu.VMEM((seq, HEAD_WIDTH), f32),
            dma((2, CHUNKS, 4)), dma((2, CHUNKS, 4)),
            dma((2, 4)), dma((2, 4)), dma((2, 4)), dma((2, 4)), dma((2, 4)), dma((2, 4)), dma((2, 4)), dma((2, 4)),
            dma((CHUNKS, n_tp)), dma((CHUNKS, n_tp)),
            dma((CHUNKS,)), dma((CHUNKS,)), dma((10,)), dma((CHUNKS,)), dma((3,)),
        ],
        compiler_params=pltpu.CompilerParams(
            collective_id=0, has_side_effects=True, vmem_limit_bytes=67043328
        ),
        name="relay",
    )(
        flight_lengths, entry_order, fresh_rows[:, 0], held, pre_gain, post_gain, jnp.asarray(cosine), jnp.asarray(sine), wq, wk, wv, wo,
    )
    return produced[None, None], received[None, None]


def solution(mesh):
    in_specs = (
        P("section", ("dp", "tp"), None, None),
        P(None, ("dp", "tp"), None, None),
        P("dp"),
        P("section", "dp"),
        P("section", None),
        P("section", None),
        P("section", None, "tp"),
        P("section", None, "tp"),
        P("section", None, "tp"),
        P("section", "tp", None),
    )
    out_specs = (P("section", ("dp", "tp"), None, None), P("section", ("dp", "tp"), None, None))
    return jax.shard_map(
        functools.partial(shards, mesh.shape["section"], mesh.shape["tp"]),
        mesh=mesh, in_specs=in_specs, out_specs=out_specs, check_vma=False,
    )
```
